32 devices in a mesh: groups: 2 (over x), rows: 16 (over z, y, core).
Axes of the slice: x: 2, y: 2, z: 4, core: 2. Of those that a mesh axis runs over, the one named last changes fastest.
Arguments:
- features: float32 [448, 14, 192], P(('groups', 'rows')), parts along dimension 0, may hold values from -6 to 6
- fine_gain_one: float32 [192], replicated, may hold values from 0.1 to 1.9
- fine_project_in: float32 [192, 576], replicated, may hold values from -30 to 30
- fine_project_out: float32 [192, 192], replicated, may hold values from -0.4375 to 0.4375
- fine_gain_two: float32 [192], replicated, may hold values from 0.1 to 1.9
- fine_expand: float32 [192, 768], replicated, may hold values from -0.4375 to 0.4375
- fine_contract: float32 [768, 192], replicated, may hold values from -0.21875 to 0.21875
- merge_gain: float32 [768], replicated, may hold values from 0.1 to 1.9
- merge_weight: float32 [768, 384], replicated, may hold values from -0.21875 to 0.21875
- coarse_gain: float32 [384], replicated, may hold values from 0.1 to 1.9
- coarse_project_in: float32 [384, 1152], replicated, may hold values from -30 to 30
- coarse_project_out: float32 [384, 384], replicated, may hold values from -0.3125 to 0.3125
- cotangent: float32 [224, 7, 384], P(('groups', 'rows')), parts along dimension 0, may hold values from -6 to 6
Outputs:
- coarse_out: float32 [224, 7, 384], P(('groups', 'rows')), parts along dimension 0
- gradient_features: float32 [448, 14, 192], P(('groups', 'rows')), parts along dimension 0
- gradient_fine_gain_one: float32 [384], P('groups'), parts along dimension 0
- gradient_fine_project_in: float32 [384, 576], P('groups'), parts along dimension 0
- gradient_fine_project_out: float32 [384, 192], P('groups'), parts along dimension 0
- gradient_fine_gain_two: float32 [384], P('groups'), parts along dimension 0
- gradient_fine_expand: float32 [384, 768], P('groups'), parts along dimension 0
- gradient_fine_contract: float32 [1536, 192], P('groups'), parts along dimension 0
- gradient_merge_gain: float32 [1536], P('groups'), parts along dimension 0
- gradient_merge_weight: float32 [1536, 384], P('groups'), parts along dimension 0
- gradient_coarse_gain: float32 [768], P('groups'), parts along dimension 0
- gradient_coarse_project_in: float32 [768, 1152], P('groups'), parts along dimension 0
- gradient_coarse_project_out: float32 [768, 384], P('groups'), parts along dimension 0
The draws below stay inside these ranges and needn't reach their ends.
There are 2 independent parts, one for each index of `groups`. The reference program is written for one: setup_inputs(seed, part) draws one part's arguments, and reference() takes and returns one part's arrays. A program takes and returns all parts, laid end to end along the dimension named above; an argument that names none is the same for every part. Nothing has to cross between parts.
All inputs are finite; a program needn't handle non-finite values.
Results may differ from the reference program's by a relative error of at most 0.0004.
Values sent between devices are 32-bit elements; how exact they have to be, the bound alone decides.
A program may use at most 128 MiB of HBM per device.

```python
import jax
import jax.numpy as jnp
from jax import lax

C_FINE = 192
HEAD_DIM = 32
FEED_UNITS = 768
W_COLS = 14
C_COARSE = 384
HT = 224


def draw_projection(key, channels):
    base = jax.random.truncated_normal(key, -4.0, 4.0, (channels, 3 * channels), jnp.float32) * channels ** (-0.5)
    return base


def draw_fine_project_in(key, part):
    return draw_projection(jax.random.fold_in(key, 11), C_FINE)


def draw_coarse_project_in(key, part):
    return draw_projection(jax.random.fold_in(key, 23), C_COARSE)


def shard_levels(own_key, dims, split, least, largest):
    def one(position, parts):
        draws = jax.random.uniform(jax.random.fold_in(jax.random.fold_in(own_key, 6), position), (parts,), jnp.float32, least / len(split), largest / len(split))
        return jnp.repeat(jnp.exp(draws), dims[position] // parts).reshape((-1,) + (1,) * (len(dims) - position - 1))

    factor_of = one(*split[0])
    for cut in split[1:]:
        factor_of = factor_of * one(*cut)
    return factor_of


def scatter_about(own_key, dims, scale, most, shards=(), held_as=jnp.bfloat16):
    loudness = shard_levels(own_key, dims, shards, -0.22, 0.18) if shards else 1.0
    values = jax.random.normal(own_key, dims, jnp.float32) * scale * loudness
    return jnp.minimum(jnp.maximum(values, -most), most).astype(held_as)


def setup_inputs(seed: int = 0, part: int = 0) -> dict:
    splits = jax.random.split(jax.random.key(seed), 14)
    part_keys = jax.random.split(jax.random.fold_in(splits[13], part), 14)
    return {
        "features": scatter_about(part_keys[0], (HT, W_COLS, C_FINE), 1.0, 6.0, ((0, 16),), jnp.float32),
        "fine_gain_one": jnp.clip(1.0 + 0.18 * jax.random.normal(splits[1], (C_FINE,), jnp.float32), 0.1, 1.9),
        "fine_project_in": draw_fine_project_in(jax.random.fold_in(splits[13], 71), part),
        "fine_project_out": scatter_about(splits[3], (C_FINE, C_FINE), C_FINE ** -0.5, 0.4375, (), jnp.float32),
        "fine_gain_two": jnp.clip(1.0 + 0.18 * jax.random.normal(splits[4], (C_FINE,), jnp.float32), 0.1, 1.9),
        "fine_expand": scatter_about(splits[5], (C_FINE, FEED_UNITS), C_FINE ** -0.5, 0.4375, (), jnp.float32),
        "fine_contract": scatter_about(splits[6], (FEED_UNITS, C_FINE), FEED_UNITS ** -0.5, 0.21875, (), jnp.float32),
        "merge_gain": jnp.clip(1.0 + 0.18 * jax.random.normal(splits[7], (4 * C_FINE,), jnp.float32), 0.1, 1.9),
        "merge_weight": scatter_about(splits[8], (4 * C_FINE, C_COARSE), (4 * C_FINE) ** -0.5, 0.21875, (), jnp.float32),
        "coarse_gain": jnp.clip(1.0 + 0.18 * jax.random.normal(splits[9], (C_COARSE,), jnp.float32), 0.1, 1.9),
        "coarse_project_in": draw_coarse_project_in(jax.random.fold_in(splits[13], 71), part),
        "coarse_project_out": scatter_about(splits[11], (C_COARSE, C_COARSE), C_COARSE ** -0.5, 0.3125, (), jnp.float32),
        "cotangent": scatter_about(part_keys[12], (HT // 2, W_COLS // 2, C_COARSE), 1.0, 6.0, ((0, 16),), jnp.float32),
    }


EPSILON = 1e-05
PRECISE = lax.Precision.HIGHEST

def layer_norm(values_in, gain_vec):
    average = lax.optimization_barrier(jnp.mean(values_in, axis=-1, keepdims=True))
    centered = values_in - average
    variance = lax.optimization_barrier(jnp.mean(centered * centered, axis=-1, keepdims=True))
    return centered * lax.rsqrt(variance + EPSILON) * gain_vec

def window_attention(window_slab, labels, weight_in, weight_out, head_size):
    slab_rows, slab_cols, channels = window_slab.shape
    head_count = channels // head_size
    win_rows = slab_rows // 7
    win_cols = slab_cols // 7
    count = win_rows * win_cols
    windows = window_slab.reshape(win_rows, 7, win_cols, 7, channels).transpose(0, 2, 1, 3, 4).reshape(count, 49, channels)
    label_win = labels.reshape(win_rows, 7, win_cols, 7).transpose(0, 2, 1, 3).reshape(count, 49)
    projected = jnp.einsum('nqc,cf->nqf', windows, weight_in, precision=PRECISE)
    projected = projected.reshape(count, 49, 3, head_count, head_size)
    queries = projected[:, :, 0]
    key_rows = projected[:, :, 1]
    value_rows = projected[:, :, 2]
    scores = jnp.einsum('nqhd,nkhd->nhqk', queries, key_rows, precision=PRECISE) * head_size ** (-0.5)
    allowed = label_win[:, None, :, None] == label_win[:, None, None, :]
    scores = jnp.where(allowed, scores, -1e+30)
    row_max = lax.optimization_barrier(jnp.max(scores, axis=-1, keepdims=True))
    weights = jnp.exp(scores - row_max)
    weights = weights / lax.optimization_barrier(jnp.sum(weights, axis=-1, keepdims=True))
    context = jnp.einsum('nhqk,nkhd->nqhd', weights, value_rows, precision=PRECISE).reshape(count, 49, channels)
    result = jnp.einsum('nqc,cf->nqf', context, weight_out, precision=PRECISE)
    return result.reshape(win_rows, win_cols, 7, 7, channels).transpose(0, 2, 1, 3, 4).reshape(slab_rows, slab_cols, channels)

def shifted_block(residual, gain_vec, project_in, project_out):
    all_rows, breadth = (residual.shape[0], residual.shape[1])
    normed = layer_norm(residual, gain_vec)
    rolled = jnp.roll(normed, (-3, -3), (0, 1))
    row_flag = (jnp.arange(all_rows) >= all_rows - 3).astype(jnp.int32)
    col_flag = (jnp.arange(breadth) >= breadth - 3).astype(jnp.int32)
    labels = row_flag[:, None] * 2 + col_flag[None, :]
    attended = window_attention(rolled, labels, project_in, project_out, HEAD_DIM)
    return residual + jnp.roll(attended, (3, 3), (0, 1))

def feed_forward(residual, gain_vec, expand, contract):
    normed = layer_norm(residual, gain_vec)
    inner = jax.nn.gelu(jnp.dot(normed, expand, precision=PRECISE), approximate=False)
    return residual + jnp.dot(inner, contract, precision=PRECISE)

def patch_merge(grid, gain_vec, weight):
    height, breadth, channels = grid.shape
    blocks = grid.reshape(height // 2, 2, breadth // 2, 2, channels).transpose(0, 2, 3, 1, 4)
    blocks = blocks.reshape(height // 2, breadth // 2, 4 * channels)
    return jnp.dot(layer_norm(blocks, gain_vec), weight, precision=PRECISE)

def forward(features, fine_gain_one, fine_project_in, fine_project_out, fine_gain_two, fine_expand, fine_contract, merge_gain, merge_weight, coarse_gain, coarse_project_in, coarse_project_out):
    fine_mid = shifted_block(features, fine_gain_one, fine_project_in, fine_project_out)
    fine_done = feed_forward(fine_mid, fine_gain_two, fine_expand, fine_contract)
    merged = patch_merge(fine_done, merge_gain, merge_weight)
    return shifted_block(merged, coarse_gain, coarse_project_in, coarse_project_out)

def reference(features, fine_gain_one, fine_project_in, fine_project_out, fine_gain_two, fine_expand, fine_contract, merge_gain, merge_weight, coarse_gain, coarse_project_in, coarse_project_out, cotangent):
    coarse_out, pullback = jax.vjp(forward, features, fine_gain_one, fine_project_in, fine_project_out, fine_gain_two, fine_expand, fine_contract, merge_gain, merge_weight, coarse_gain, coarse_project_in, coarse_project_out)
    grads = pullback(cotangent)
    grad_scale = 1.0 / jnp.sqrt(jnp.float32(coarse_out.shape[0] * coarse_out.shape[1]))
    scaled = [grads[index] * grad_scale for index in range(1, 12)]
    return (coarse_out, grads[0], scaled[0], scaled[1], scaled[2], scaled[3], scaled[4], scaled[5], scaled[6], scaled[7], scaled[8], scaled[9], scaled[10])
```

```python
import functools

import jax
import jax.numpy as jnp
from jax import lax
from jax.experimental import pallas as pl
from jax.experimental.pallas import tpu as pltpu
from jax.sharding import PartitionSpec as P

HEAD_DIM = 32
WIN = 7
PAD = 8
TOK = PAD * PAD
SHIFT = 3
EPSILON = 1e-05
MESH = pl.DeviceIdType.MESH
F32 = jnp.float32
BF16 = jnp.bfloat16
NN = (((1,), (0,)), ((), ()))
NT = (((1,), (1,)), ((), ()))
TN = (((0,), (0,)), ((), ()))


def halves(a):
    hi = a.astype(BF16)
    return hi, (a - hi.astype(F32)).astype(BF16)


def mm(a, b, dims=NN):
    a = a if isinstance(a, tuple) else halves(a)
    b = b if isinstance(b, tuple) else halves(b)
    dot = functools.partial(lax.dot_general, dimension_numbers=dims, preferred_element_type=F32)
    return dot(a[0], b[0]) + (dot(a[0], b[1]) + dot(a[1], b[0]))


def runs(first, count, breadth):
    head = min(count, breadth - first % breadth)
    pieces = [(0, first % breadth, head)]
    return pieces + ([(head, 0, count - head)] if head < count else [])


def fill_windows(dst, row_of, win_row, win_cols, breadth):
    for col in range(win_cols):
        for i in range(WIN):
            ref, at = row_of(win_row * WIN + i)
            for place, start, size in runs(col * WIN + SHIFT, WIN, breadth):
                dst[win_row * win_cols + col, i, place : place + size, :] = ref[at, start : start + size, :]


def put_windows(dst, top, src, win_row, win_cols):
    breadth = dst.shape[1]
    for col in range(win_cols):
        for place, start, size in runs(col * WIN + SHIFT, WIN, breadth):
            dst[top : top + WIN, start : start + size, :] = src[
                win_row * win_cols + col, :WIN, place : place + size, :
            ]


def norm(v):
    centered = v - jnp.mean(v, axis=-1, keepdims=True)
    scale = lax.rsqrt(jnp.mean(centered * centered, axis=-1, keepdims=True) + EPSILON)
    return centered * scale, scale


def norm_back(dn, n, scale):
    return scale * (
        dn - jnp.mean(dn, axis=-1, keepdims=True) - n * jnp.mean(dn * n, axis=-1, keepdims=True)
    )


def spread(a, heads):
    lane = lax.broadcasted_iota(jnp.int32, a.shape, 1) // HEAD_DIM
    return jnp.concatenate([jnp.where(lane == h, a, 0.0) for h in range(heads)], axis=0)


def gather_heads(a, heads):
    rows = a.shape[0] // heads
    lane = lax.broadcasted_iota(jnp.int32, (rows, a.shape[1]), 1) // HEAD_DIM
    total = jnp.where(lane == 0, a[:rows], 0.0)
    for h in range(1, heads):
        total = jnp.where(lane == h, a[h * rows : (h + 1) * rows], total)
    return total


def allowed(last_row, last_col):
    def label(axis):
        t = lax.broadcasted_iota(jnp.int32, (TOK, TOK), axis)
        r, c = t // PAD, t % PAD
        lab = jnp.where(r >= WIN - SHIFT, last_row * 2, 0) + jnp.where(
            c >= WIN - SHIFT, last_col, 0
        )
        return lab, (r < WIN) & (c < WIN)

    lq, _ = label(0)
    lk, real = label(1)
    return (lq == lk) & real


def attend(q, k, v, mask, heads):
    s = mm(spread(q, heads), k, NT) * HEAD_DIM**-0.5
    s = jnp.where(jnp.concatenate([mask] * heads, axis=0), s, -1e30)
    w = jnp.exp(s - jnp.max(s, axis=-1, keepdims=True))
    w = w / jnp.sum(w, axis=-1, keepdims=True)
    return w, gather_heads(mm(w, v), heads)


def attend_back(dctx, q, k, v, w, heads):
    dc = halves(spread(dctx, heads))
    dw = mm(dc, v, NT)
    dv = mm(w, dc, TN)
    ds = w * (dw - jnp.sum(dw * w, axis=-1, keepdims=True)) * HEAD_DIM**-0.5
    ds = halves(ds)
    dq = gather_heads(mm(ds, k), heads)
    dk = mm(ds, spread(q, heads), TN)
    return dq, dk, dv


LOADS = ("features", "fine_in", "fine_out", "cotangent", "expand", "contract", "merge", "coarse_in", "coarse_out")


class Ring:
    def __init__(self, chips, rounds, g, out, pair_buf, acc, ring_buf, sems):
        self.chips, self.rounds = chips, rounds
        self.g, self.out, self.pair_buf, self.acc, self.ring_buf = g, out, pair_buf, acc, ring_buf
        (self.pair_send, self.pair_recv, self.rs_send, self.rs_recv, self.ag_send, self.ag_recv, self.back_send, self.back_recv) = sems
        me = lax.axis_index("rows")
        self.core, chip = me % 2, me // 2
        column, line = chip % 2, chip // 2
        self.at = jnp.where(column == 0, line, chips - 1 - line)
        self.step = 1 - 2 * self.core
        self.ahead, self.behind = self.device(self.at + self.step), self.device(self.at - self.step)
        self.mate = me + 1 - 2 * self.core

    def device(self, q):
        chips = self.chips
        q = (q + chips) % chips
        return jnp.where(q < chips // 2, q * 2, (chips - 1 - q) * 2 + 1) * 2 + self.core

    def slot(self, r, chunk):
        top, seg = self.rounds[r]
        chunk = (chunk + 2 * self.chips) % self.chips
        return pl.ds(pl.multiple_of(top // 2 + chunk * seg, 8), seg)

    def rows(self, r, half, chunk):
        top, seg = self.rounds[r]
        chunk = (chunk + 2 * self.chips) % self.chips
        return pl.ds(pl.multiple_of(top + (half * self.chips + chunk) * seg, 8), seg)

    def landing(self, r, s):
        top, seg = self.rounds[r]
        return pl.ds(top // 2 + s * seg, seg)

    def remote(self, src, dst, send, recv, target):
        return pltpu.make_async_remote_copy(
            src_ref=src, dst_ref=dst, send_sem=send, recv_sem=recv, device_id={"rows": target}, device_id_type=MESH
        )

    def pair_copy(self, r, s, sign=1):
        chunk = self.at + sign * self.step * s
        return self.remote(
            self.g.at[self.rows(r, 1 - self.core, chunk)],
            self.pair_buf.at[self.slot(r, chunk)],
            self.pair_send.at[r, s],
            self.pair_recv.at[r, s],
            self.mate,
        )

    def rs_copy(self, r, s):
        return self.remote(
            self.acc.at[self.slot(r, self.at - self.step * s)],
            self.ring_buf.at[self.landing(r, s)],
            self.rs_send.at[r, s],
            self.rs_recv.at[r, s],
            self.ahead,
        )

    def ag_copy(self, r, s, shift):
        where = self.rows(r, self.core, self.at + shift * self.step - self.step * s)
        return self.remote(self.out.at[where], self.out.at[where], self.ag_send.at[r, s], self.ag_recv.at[r, s], self.ahead)

    def back_copy(self, r, s):
        where = self.rows(r, self.core, self.at + self.step - self.step * s)
        return self.remote(self.out.at[where], self.out.at[where], self.back_send.at[r, s], self.back_recv.at[r, s], self.mate)

    def back_arrival(self, r, s):
        where = self.rows(r, 1 - self.core, self.at - self.step + self.step * s)
        return self.remote(self.out.at[where], self.out.at[where], self.back_send.at[r, s], self.back_recv.at[r, s], self.mate)

    def launch(self, r):
        for s in range(self.chips):
            self.pair_copy(r, s).start()

    def advance(self, r, s):
        chips = self.chips
        if s < chips:
            chunk = self.at - self.step * s
            self.pair_copy(r, s, -1).wait_recv()
            total = self.g[self.rows(r, self.core, chunk), :] + self.pair_buf[self.slot(r, chunk), :]
            if s > 0:
                self.rs_copy(r, s - 1).wait_recv()
                total = total + self.ring_buf[self.landing(r, s - 1), :]
            if s < chips - 1:
                self.acc[self.slot(r, chunk), :] = total
                self.rs_copy(r, s).start()
            else:
                self.out[self.rows(r, self.core, chunk), :] = total
                self.ag_copy(r, 0, 1).start()
                self.back_copy(r, 0).start()
        else:
            s -= chips
            self.ag_copy(r, s, 0).wait_recv()
            if s < chips - 2:
                self.ag_copy(r, s + 1, 1).start()
            self.back_copy(r, s + 1).start()

    def finish(self, r):
        for s in range(self.chips):
            self.pair_copy(r, s).wait_send()
            self.back_copy(r, s).wait_send()
            self.back_arrival(r, s).wait_recv()
            if s < self.chips - 1:
                self.rs_copy(r, s).wait_send()
                self.ag_copy(r, s, 1).wait_send()


def whole_step(
    grad_scale, chips, spot, rounds, win_cols,
    features, fine_in, fine_out, cotangent, expand, contract, merge, coarse_in, coarse_out,
    g1_ref, g2_ref, gm_ref, gc_ref,
    out_ref, dx_ref, sum_ref,
    f_ref, fin, fout, cot_ref, we, wc, wm, cin, cout,
    f_halo, cot_halo, mid_halo, prefix,
    cells, x_ref, qkv_ref, w_ref, ctx_ref, dqkv_ref, d_all,
    mid_ref, dmid_ref, out_frame, dx_frame, coarse_cells, quads, h_ref, act_ref,
    pack_ref, pair_buf, acc, ring_buf,
    load_sem, halo_send, halo_recv, local_sem, *ring_sems,
):
    height, breadth, cf = f_ref.shape
    cc = cot_ref.shape[2]
    low = cot_ref.shape[0]
    heads, coarse_heads = cf // HEAD_DIM, cc // HEAD_DIM
    win_rows = height // WIN
    n = 2 * chips
    me = lax.axis_index("rows")
    above, below = (me + n - 1) % n, (me + 1) % n
    last = (me == n - 1).astype(jnp.int32)

    sources = (features, fine_in, fine_out, cotangent, expand, contract, merge, coarse_in, coarse_out)
    targets = (f_ref, fin, fout, cot_ref, we, wc, wm, cin, cout)
    loads = {
        name: pltpu.make_async_copy(src, dst, load_sem.at[i])
        for i, (name, src, dst) in enumerate(zip(LOADS, sources, targets))
    }
    for name in LOADS:
        loads[name].start()

    ring = Ring(chips, rounds, pack_ref, sum_ref, pair_buf, acc, ring_buf, ring_sems)
    barrier = pltpu.get_barrier_semaphore()
    for other in (above, below, ring.ahead, ring.behind, ring.mate):
        pl.semaphore_signal(barrier, inc=1, device_id={"rows": other}, device_id_type=MESH)
    pl.semaphore_wait(barrier, 5)

    def halo(i, src, dst, target):
        return ring.remote(src, dst, halo_send.at[i], halo_recv.at[i], target)

    send_f = halo(0, features.at[pl.ds(0, SHIFT)], f_halo, above)
    send_cot = halo(1, cotangent.at[pl.ds(0, SHIFT)], cot_halo, above)
    send_mid = halo(2, mid_ref.at[pl.ds(0, SHIFT)], mid_halo, above)
    send_out = halo(3, out_frame.at[pl.ds(low - SHIFT, SHIFT)], out_ref.at[pl.ds(0, SHIFT)], below)
    send_dmid = halo(4, dmid_ref.at[pl.ds(height - SHIFT, SHIFT)], prefix, below)
    send_dx = halo(5, dx_frame.at[pl.ds(height - SHIFT, SHIFT)], dx_ref.at[pl.ds(0, SHIFT)], below)
    send_f.start()
    send_cot.start()

    cells[...] = jnp.zeros_like(cells)
    quads[...] = jnp.zeros_like(quads)
    g1 = g1_ref[...].reshape(1, cf)
    rows_per = win_cols * TOK

    def window_mask(win_row, col):
        return allowed(last if win_row == win_rows - 1 else 0, int(col == win_cols - 1))

    loads["features"].wait()
    for wr in range(win_rows):
        if wr == win_rows - 1:
            send_f.wait_recv()
        fill_windows(
            cells,
            lambda r: (f_ref, r + SHIFT) if r + SHIFT < height else (f_halo, r + SHIFT - height),
            wr, win_cols, breadth,
        )
        at = slice(wr * rows_per, (wr + 1) * rows_per)
        x = cells[wr * win_cols : (wr + 1) * win_cols].reshape(rows_per, cf)
        x_ref[at, :] = x
        unit, _ = norm(x)
        u = halves(unit * g1)
        if wr == 0:
            loads["fine_in"].wait()
        parts = []
        for part in range(3):
            got = mm(u, fin[:, part * cf : (part + 1) * cf])
            qkv_ref[part, at, :] = got
            parts.append(got)
        for col in range(win_cols):
            i = wr * win_cols + col
            inside = slice(col * TOK, (col + 1) * TOK)
            w, ctx = attend(parts[0][inside], parts[1][inside], parts[2][inside], window_mask(wr, col), heads)
            w_ref[i] = w
            ctx_ref[i * TOK : (i + 1) * TOK, :] = ctx
        if wr == 0:
            loads["fine_out"].wait()
        mid = x + mm(ctx_ref[at, :], fout[...])
        cells[wr * win_cols : (wr + 1) * win_cols] = mid.reshape(win_cols, PAD, PAD, cf)
        put_windows(mid_ref, wr * WIN, cells, wr, win_cols)
        if wr == 0:
            send_mid.start()

    g2 = g2_ref[...].reshape(1, cf)
    gmv = gm_ref[...].reshape(1, 4 * cf)
    gm = [gmv[:, k * cf : (k + 1) * cf] for k in range(4)]
    gc = gc_ref[...].reshape(1, cc)
    send_mid.wait_recv()
    for k in range(4):
        dj, di = divmod(k, 2)
        for i in range(WIN):
            r = SHIFT + 2 * i + di
            ref, r = (mid_ref, r) if r < height else (mid_halo, r - height)
            for j in range(WIN):
                at = (2 * (SHIFT + j) + dj) % breadth
                quads[k, i, j : j + 1, :] = ref[r, at : at + 1, :]
    x = quads[...].reshape(4 * TOK, cf)
    n2, r2 = norm(x)
    u2 = halves(n2 * g2)
    loads["expand"].wait()
    h = mm(u2, we[...])
    h_ref[...] = h
    act = h * (0.5 * (1.0 + lax.erf(h * 0.5**0.5)))
    act_ref[...] = act
    loads["contract"].wait()
    y = x + mm(act, wc[...], NT)
    ys = [y[k * TOK : (k + 1) * TOK] for k in range(4)]
    wide = 1.0 / (4 * cf)
    mean = sum(jnp.sum(v, axis=-1, keepdims=True) for v in ys) * wide
    ys = [v - mean for v in ys]
    rm = lax.rsqrt(sum(jnp.sum(v * v, axis=-1, keepdims=True) for v in ys) * wide + EPSILON)
    nm = [v * rm for v in ys]
    um = [halves(nm[k] * gm[k]) for k in range(4)]
    loads["merge"].wait()
    merged = sum(mm(um[k], wm[k * cf : (k + 1) * cf, :]) for k in range(4))
    nc, rc = norm(merged)
    uc = halves(nc * gc)
    loads["coarse_in"].wait()
    q, k_, v_ = (mm(uc, cin[:, p * cc : (p + 1) * cc]) for p in range(3))
    w, ctx = attend(q, k_, v_, allowed(last, 1), coarse_heads)
    loads["coarse_out"].wait()
    coarse_cells[0] = (merged + mm(ctx, cout[...])).reshape(PAD, PAD, cc)
    put_windows(out_frame, 0, coarse_cells, 0, 1)
    send_out.start()

    loads["cotangent"].wait()
    send_cot.wait_recv()
    coarse_cells[...] = jnp.zeros_like(coarse_cells)
    fill_windows(
        coarse_cells,
        lambda r: (cot_ref, r + SHIFT) if r + SHIFT < low else (cot_halo, r + SHIFT - low),
        0, 1, low,
    )
    cot = coarse_cells[0].reshape(TOK, cc)
    ch = halves(cot)
    pack_ref[spot["coarse_out"] : spot["coarse_out"] + cc, :] = mm(ctx, ch, TN) * grad_scale
    dctx = mm(ch, cout[...], NT)
    got = attend_back(dctx, q, k_, v_, w, coarse_heads)
    du = 0.0
    for p in range(3):
        dp = halves(got[p])
        top = spot["coarse_in", p]
        pack_ref[top : top + cc, :] = mm(uc, dp, TN) * grad_scale
        du += mm(dp, cin[:, p * cc : (p + 1) * cc], NT)
        if p == 0:
            ring.launch(0)
    ring.launch(1)
    ring.advance(0, 0)
    gains = spot["gains"]
    pack_ref[gains:, :] = jnp.zeros_like(pack_ref[gains:, :])
    pack_ref[gains + 3 : gains + 4, :] = jnp.sum(du * nc, axis=0, keepdims=True) * grad_scale
    dm = cot + norm_back(du * gc, nc, rc)
    mh = halves(dm)
    dn = []
    for k in range(4):
        top = spot["merge"] + k * cf
        pack_ref[top : top + cf, :] = mm(um[k], mh, TN) * grad_scale
        dk = mm(mh, wm[k * cf : (k + 1) * cf, :], NT)
        row = gains + 1 + k // 2
        pack_ref[row : row + 1, (k % 2) * cf : (k % 2 + 1) * cf] = jnp.sum(dk * nm[k], axis=0, keepdims=True) * grad_scale
        dn.append(dk * gm[k])
    ring.launch(2)
    ring.advance(1, 0)
    ring.advance(0, 1)
    m1 = sum(jnp.sum(v, axis=-1, keepdims=True) for v in dn) * wide
    m2 = sum(jnp.sum(dn[k] * nm[k], axis=-1, keepdims=True) for k in range(4)) * wide
    dy = jnp.concatenate([rm * (dn[k] - m1 - nm[k] * m2) for k in range(4)], axis=0)
    yh = halves(dy)
    dwc = mm(yh, act_ref[...], TN) * grad_scale
    top = spot["contract"]
    for p in range(dwc.shape[1] // cc):
        pack_ref[top + p * cf : top + (p + 1) * cf, :] = dwc[:, p * cc : (p + 1) * cc]
    ring.advance(2, 0)
    ring.advance(1, 1)
    ring.advance(0, 2)
    h = h_ref[...]
    slope = 0.5 * (1.0 + lax.erf(h * 0.5**0.5)) + h * (jnp.exp(-0.5 * h * h) * 0.3989422804014327)
    dh = halves(mm(yh, wc[...]) * slope)
    dwe = mm(u2, dh, TN) * grad_scale
    top = spot["expand"]
    for p in range(dwe.shape[1] // cc):
        pack_ref[top + p * cf : top + (p + 1) * cf, :] = dwe[:, p * cc : (p + 1) * cc]
    ring.launch(3)
    du2 = mm(dh, we[...], NT)
    pack_ref[gains : gains + 1, :cf] = jnp.sum(du2 * n2, axis=0, keepdims=True) * grad_scale
    quads[...] = (dy + norm_back(du2 * g2, n2, r2)).reshape(quads.shape)
    for k in range(4):
        dj, di = divmod(k, 2)
        for i in range(WIN):
            for j in range(WIN):
                at = (2 * (SHIFT + j) + dj) % breadth
                dmid_ref[2 * i + di, at : at + 1, :] = quads[k, i, j : j + 1, :]
    send_dmid.start()
    ring.advance(3, 0)
    ring.advance(2, 1)
    ring.advance(1, 2)
    ring.advance(0, 3)

    for w0 in range(cells.shape[0]):
        cells[w0, WIN:, :, :] = jnp.zeros_like(cells[w0, WIN:, :, :])
        cells[w0, :, WIN:, :] = jnp.zeros_like(cells[w0, :, WIN:, :])
    for wr in reversed(range(win_rows)):
        if wr == 0:
            send_dmid.wait_recv()
        fill_windows(
            cells, lambda r: (dmid_ref, r - SHIFT) if r >= SHIFT else (prefix, r), wr, win_cols, breadth
        )
        at = slice(wr * rows_per, (wr + 1) * rows_per)
        d = cells[wr * win_cols : (wr + 1) * win_cols].reshape(rows_per, cf)
        d_all[at, :] = d
        unit, scale = norm(x_ref[at, :])
        dctx = mm(d, fout[...], NT)
        for col in range(win_cols):
            i = wr * win_cols + col
            inside = slice(i * TOK, (i + 1) * TOK)
            got = attend_back(
                dctx[col * TOK : (col + 1) * TOK], qkv_ref[0, inside, :], qkv_ref[1, inside, :], qkv_ref[2, inside, :], w_ref[i], heads
            )
            for part in range(3):
                dqkv_ref[part, inside, :] = got[part]
        du = 0.0
        for part in range(3):
            du += mm(dqkv_ref[part, at, :], fin[:, part * cf : (part + 1) * cf], NT)
        gain_part = jnp.sum(du * unit, axis=0, keepdims=True)
        gain_one = gain_part if wr == win_rows - 1 else gain_one + gain_part
        cells[wr * win_cols : (wr + 1) * win_cols] = (d + norm_back(du * g1, unit, scale)).reshape(win_cols, PAD, PAD, cf)
        put_windows(dx_frame, wr * WIN, cells, wr, win_cols)
        if wr == win_rows - 1:
            send_dx.start()
        shift = win_rows - 1 - wr
        for r in range(4):
            ring.advance(3 - r, 1 + shift + r)
    unit, _ = norm(x_ref[...])
    u = halves(unit * g1)
    weight = [mm(u, dqkv_ref[part], TN) * grad_scale for part in range(3)]
    dwout = mm(ctx_ref[...], d_all[...], TN) * grad_scale
    top = spot["fine"]
    pack_ref[top : top + cf, :] = jnp.concatenate(weight[:2], axis=1)
    pack_ref[top + cf : top + 2 * cf, :] = jnp.concatenate([weight[2], dwout], axis=1)
    pack_ref[gains + 4 : gains + 5, :cf] = gain_one * grad_scale
    ring.launch(4)

    keep_out = pltpu.make_async_copy(
        out_frame.at[pl.ds(0, low - SHIFT)], out_ref.at[pl.ds(SHIFT, low - SHIFT)], local_sem.at[0]
    )
    keep_dx = pltpu.make_async_copy(
        dx_frame.at[pl.ds(0, height - SHIFT)], dx_ref.at[pl.ds(SHIFT, height - SHIFT)], local_sem.at[1]
    )
    keep_out.start()
    keep_dx.start()
    count = len(rounds)
    starts = [0, 1, 2, 3, 5]
    done = [1 + win_rows + 3 - r for r in range(4)] + [0]
    steps = 2 * chips - 1
    todo = sorted(
        (s + starts[r], r, s) for r in range(count) for s in range(done[r], steps)
    )
    for _, r, s in todo:
        ring.advance(r, s)
    for r in range(count):
        ring.finish(r)
    keep_out.wait()
    keep_dx.wait()
    for copy in (send_f, send_cot, send_mid, send_out, send_dmid, send_dx):
        copy.wait_send()
    send_out.wait_recv()
    send_dx.wait_recv()


def unpack(spot, cf, cc, sum_ref, out_ref, dx_ref, *rest):
    (coarse_out, grad_features, g1, fine_in, fine_out, g2, expand, contract, gm, merge, gc, coarse_in, coarse_proj) = rest[:13]
    sems = rest[13]
    moves = [
        (out_ref, coarse_out),
        (dx_ref, grad_features),
        (sum_ref.at[pl.ds(spot["merge"], 4 * cf)], merge),
        (sum_ref.at[pl.ds(spot["coarse_out"], cc)], coarse_proj),
    ]
    for name, into in (("coarse_in", coarse_in), ("expand", expand), ("contract", contract)):
        size = into.shape[0]
        for p in range(into.shape[1] // cc):
            at = spot[name, p] if (name, p) in spot else spot[name] + p * size
            moves.append((sum_ref.at[pl.ds(at, size)], into.at[:, pl.ds(p * cc, cc)]))
    copies = [pltpu.make_async_copy(src, dst, sems.at[i]) for i, (src, dst) in enumerate(moves)]
    for copy in copies:
        copy.start()
    top = spot["fine"]
    fine_in[:, :cc] = sum_ref[top : top + cf, :]
    fine_in[:, cc:] = sum_ref[top + cf : top + 2 * cf, :cf]
    fine_out[...] = sum_ref[top + cf : top + 2 * cf, cf:]
    gains = spot["gains"]
    g1[...] = sum_ref[gains + 4 : gains + 5, :cf].reshape(g1.shape)
    g2[...] = sum_ref[gains : gains + 1, :cf].reshape(g2.shape)
    gm[...] = jnp.concatenate([sum_ref[gains + 1 : gains + 2, :], sum_ref[gains + 2 : gains + 3, :]], axis=1).reshape(gm.shape)
    gc[...] = sum_ref[gains + 3 : gains + 4, :].reshape(gc.shape)
    for copy in copies:
        copy.wait()


def shards(
    features,
    fine_gain_one,
    fine_project_in,
    fine_project_out,
    fine_gain_two,
    fine_expand,
    fine_contract,
    merge_gain,
    merge_weight,
    coarse_gain,
    coarse_project_in,
    coarse_project_out,
    cotangent,
):
    devices = lax.axis_size("rows")
    chips = devices // 2
    height, breadth, cf = features.shape
    low, narrow, cc = cotangent.shape
    units = fine_expand.shape[1]
    assert low == narrow == WIN and cc == 2 * cf and units % cc == 0
    grad_scale = 1.0 / (devices * low * narrow) ** 0.5
    win_rows, win_cols = height // WIN, breadth // WIN
    count = win_rows * win_cols
    heads = cf // HEAD_DIM
    tokens = count * TOK
    vmem = pl.BlockSpec(memory_space=pltpu.VMEM)
    anywhere = pl.BlockSpec(memory_space=pl.ANY)

    def shape(*dims):
        return jax.ShapeDtypeStruct(dims, F32)

    def limit(mib):
        return pltpu.CompilerParams(vmem_limit_bytes=mib * 2**20)

    grain = 8 * devices
    spot, rounds, rows = {}, [], 0
    strips = units // cc * cf
    plan = (
        (("coarse_out", cc), (("coarse_in", 0), cc)),
        ((("coarse_in", 1), cc), (("coarse_in", 2), cc)),
        (("merge", 4 * cf),),
        (("contract", strips), ("expand", strips)),
        (("fine", 2 * cf), ("gains", 8)),
    )
    for group in plan:
        top = rows
        for name, size in group:
            spot[name] = rows
            rows += size
        padded = -(-(rows - top) // grain) * grain
        rounds.append((top, padded // devices))
        rows = top + padded
    total = rows
    scratch = [
        pltpu.VMEM(a.shape, F32)
        for a in (
            features, fine_project_in, fine_project_out, cotangent, fine_expand, fine_expand, merge_weight, coarse_project_in, coarse_project_out,
        )
    ]
    scratch += [
        pltpu.VMEM(dims, F32)
        for dims in (
            (SHIFT, breadth, cf),
            (SHIFT, narrow, cc),
            (SHIFT, breadth, cf),
            (SHIFT, breadth, cf),
            (count, PAD, PAD, cf),
            (tokens, cf),
            (3, tokens, cf),
            (count, heads * TOK, TOK),
            (tokens, cf),
            (3, tokens, cf),
            (tokens, cf),
            (height, breadth, cf),
            (height, breadth, cf),
            (low, narrow, cc),
            (height, breadth, cf),
            (1, PAD, PAD, cc),
            (4, PAD, PAD, cf),
            (4 * TOK, units),
            (4 * TOK, units),
            (total, cc),
            (total // 2, cc),
            (total // 2, cc),
            (total // 2, cc),
        )
    ]
    dma = pltpu.SemaphoreType.DMA
    scratch += [dma((len(LOADS),)), dma((6,)), dma((6,)), dma((2,))]
    scratch += [dma((len(rounds), chips)) for _ in range(8)]
    out_slab, dx, summed = pl.pallas_call(
        functools.partial(whole_step, grad_scale, chips, spot, rounds, win_cols),
        out_shape=(shape(low, narrow, cc), shape(height, breadth, cf), shape(total, cc)),
        in_specs=[anywhere] * 9 + [vmem] * 4,
        out_specs=(vmem,) * 3,
        scratch_shapes=scratch,
        compiler_params=pltpu.CompilerParams(
            collective_id=0, has_side_effects=True, vmem_limit_bytes=50 * 2**20
        ),
        name="whole_step",
    )(
        features, fine_project_in, fine_project_out, cotangent, fine_expand, fine_contract.T, merge_weight, coarse_project_in, coarse_project_out,
        fine_gain_one, fine_gain_two, merge_gain, coarse_gain,
    )
    final = pl.pallas_call(
        functools.partial(unpack, spot, cf, cc),
        out_shape=(
            shape(low, narrow, cc),
            shape(height, breadth, cf),
            shape(cf),
            shape(cf, 3 * cf),
            shape(cf, cf),
            shape(cf),
            shape(cf, units),
            shape(cf, units),
            shape(4 * cf),
            shape(4 * cf, cc),
            shape(cc),
            shape(cc, 3 * cc),
            shape(cc, cc),
        ),
        in_specs=[vmem] * 3,
        out_specs=(anywhere, anywhere, vmem, vmem, vmem, vmem, anywhere, anywhere, vmem, anywhere, vmem, anywhere, anywhere),
        scratch_shapes=[pltpu.SemaphoreType.DMA((4 + 3 + 2 * (units // cc),))],
        compiler_params=limit(20),
        name="unpack",
    )(summed, out_slab, dx)
    final = list(final)
    final[7] = final[7].T
    return tuple(final)


def solution(mesh):
    tokens = P(("groups", "rows"), None, None)
    vector, matrix = P("groups"), P("groups", None)
    in_specs = (tokens,) + (P(),) * 11 + (tokens,)
    out_specs = (
        tokens,
        tokens,
        vector,
        matrix,
        matrix,
        vector,
        matrix,
        matrix,
        vector,
        matrix,
        vector,
        matrix,
        matrix,
    )
    return jax.shard_map(shards, mesh=mesh, in_specs=in_specs, out_specs=out_specs, check_vma=False)
```

```python
import functools

import jax
import jax.numpy as jnp
from jax import lax
from jax.experimental import pallas as pl
from jax.experimental.pallas import tpu as pltpu
from jax.sharding import PartitionSpec as P

HEAD_DIM = 32
WIN = 7
PAD = 8
TOK = PAD * PAD
SHIFT = 3
EPSILON = 1e-05
MESH = pl.DeviceIdType.MESH
F32 = jnp.float32
BF16 = jnp.bfloat16
NN = (((1,), (0,)), ((), ()))
NT = (((1,), (1,)), ((), ()))
TN = (((0,), (0,)), ((), ()))


def halves(a):
    hi = a.astype(BF16)
    return hi, (a - hi.astype(F32)).astype(BF16)


def mm(a, b, dims=NN):
    a = a if isinstance(a, tuple) else halves(a)
    b = b if isinstance(b, tuple) else halves(b)
    dot = functools.partial(lax.dot_general, dimension_numbers=dims, preferred_element_type=F32)
    return dot(a[0], b[0]) + (dot(a[0], b[1]) + dot(a[1], b[0]))


def runs(first, count, breadth):
    head = min(count, breadth - first % breadth)
    pieces = [(0, first % breadth, head)]
    return pieces + ([(head, 0, count - head)] if head < count else [])


def fill_windows(dst, row_of, win_row, win_cols, breadth):
    for col in range(win_cols):
        for i in range(WIN):
            ref, at = row_of(win_row * WIN + i)
            for place, start, size in runs(col * WIN + SHIFT, WIN, breadth):
                dst[win_row * win_cols + col, i, place : place + size, :] = ref[at, start : start + size, :]


def put_windows(dst, top, src, win_row, win_cols):
    breadth = dst.shape[1]
    for col in range(win_cols):
        for place, start, size in runs(col * WIN + SHIFT, WIN, breadth):
            dst[top : top + WIN, start : start + size, :] = src[
                win_row * win_cols + col, :WIN, place : place + size, :
            ]


def norm(v):
    centered = v - jnp.mean(v, axis=-1, keepdims=True)
    scale = lax.rsqrt(jnp.mean(centered * centered, axis=-1, keepdims=True) + EPSILON)
    return centered * scale, scale


def norm_back(dn, n, scale):
    return scale * (
        dn - jnp.mean(dn, axis=-1, keepdims=True) - n * jnp.mean(dn * n, axis=-1, keepdims=True)
    )


def spread(a, heads):
    lane = lax.broadcasted_iota(jnp.int32, a.shape, 1) // HEAD_DIM
    return jnp.concatenate([jnp.where(lane == h, a, 0.0) for h in range(heads)], axis=0)


def gather_heads(a, heads):
    rows = a.shape[0] // heads
    lane = lax.broadcasted_iota(jnp.int32, (rows, a.shape[1]), 1) // HEAD_DIM
    total = jnp.where(lane == 0, a[:rows], 0.0)
    for h in range(1, heads):
        total = jnp.where(lane == h, a[h * rows : (h + 1) * rows], total)
    return total


def allowed(last_row, last_col):
    def label(axis):
        t = lax.broadcasted_iota(jnp.int32, (TOK, TOK), axis)
        r, c = t // PAD, t % PAD
        lab = jnp.where(r >= WIN - SHIFT, last_row * 2, 0) + jnp.where(
            c >= WIN - SHIFT, last_col, 0
        )
        return lab, (r < WIN) & (c < WIN)

    lq, _ = label(0)
    lk, real = label(1)
    return (lq == lk) & real


def attend(q, k, v, mask, heads):
    s = mm(spread(q, heads), k, NT) * HEAD_DIM**-0.5
    s = jnp.where(jnp.concatenate([mask] * heads, axis=0), s, -1e30)
    w = jnp.exp(s - jnp.max(s, axis=-1, keepdims=True))
    w = w / jnp.sum(w, axis=-1, keepdims=True)
    return w, gather_heads(mm(w, v), heads)


def attend_back(dctx, q, k, v, w, heads):
    dc = halves(spread(dctx, heads))
    dw = mm(dc, v, NT)
    dv = mm(w, dc, TN)
    ds = w * (dw - jnp.sum(dw * w, axis=-1, keepdims=True)) * HEAD_DIM**-0.5
    ds = halves(ds)
    dq = gather_heads(mm(ds, k), heads)
    dk = mm(ds, spread(q, heads), TN)
    return dq, dk, dv


LOADS = (
    "features", "g1", "fine_in", "fine_out", "g2", "expand", "contract", "gm", "merge", "gc", "coarse_in", "coarse_out", "cotangent",
)


class Ring:
    def __init__(self, chips, rounds, g, out, pair_buf, acc, ring_buf, sems):
        self.chips, self.rounds = chips, rounds
        self.g, self.out, self.pair_buf, self.acc, self.ring_buf = g, out, pair_buf, acc, ring_buf
        (self.pair_send, self.pair_recv, self.rs_send, self.rs_recv, self.ag_send, self.ag_recv, self.back_send, self.back_recv) = sems
        me = lax.axis_index("rows")
        self.core, chip = me % 2, me // 2
        column, line = chip % 2, chip // 2
        self.at = jnp.where(column == 0, line, chips - 1 - line)
        self.step = 1 - 2 * self.core
        self.ahead, self.behind = self.device(self.at + self.step), self.device(self.at - self.step)
        self.mate = me + 1 - 2 * self.core

    def device(self, q):
        chips = self.chips
        q = (q + chips) % chips
        return jnp.where(q < chips // 2, q * 2, (chips - 1 - q) * 2 + 1) * 2 + self.core

    def slot(self, r, chunk):
        top, seg = self.rounds[r]
        chunk = (chunk + 2 * self.chips) % self.chips
        return pl.ds(pl.multiple_of(top // 2 + chunk * seg, 8), seg)

    def rows(self, r, half, chunk):
        top, seg = self.rounds[r]
        chunk = (chunk + 2 * self.chips) % self.chips
        return pl.ds(pl.multiple_of(top + (half * self.chips + chunk) * seg, 8), seg)

    def landing(self, r, s):
        top, seg = self.rounds[r]
        return pl.ds(top // 2 + s * seg, seg)

    def remote(self, src, dst, send, recv, target):
        return pltpu.make_async_remote_copy(
            src_ref=src, dst_ref=dst, send_sem=send, recv_sem=recv, device_id={"rows": target}, device_id_type=MESH
        )

    def pair_copy(self, r, s, sign=1):
        chunk = self.at + sign * self.step * s
        return self.remote(
            self.g.at[self.rows(r, 1 - self.core, chunk)],
            self.pair_buf.at[self.slot(r, chunk)],
            self.pair_send.at[r, s],
            self.pair_recv.at[r, s],
            self.mate,
        )

    def rs_copy(self, r, s):
        return self.remote(
            self.acc.at[self.slot(r, self.at - self.step * s)],
            self.ring_buf.at[self.landing(r, s)],
            self.rs_send.at[r, s],
            self.rs_recv.at[r, s],
            self.ahead,
        )

    def ag_copy(self, r, s, shift):
        where = self.rows(r, self.core, self.at + shift * self.step - self.step * s)
        return self.remote(self.out.at[where], self.out.at[where], self.ag_send.at[r, s], self.ag_recv.at[r, s], self.ahead)

    def back_copy(self, r, s):
        where = self.rows(r, self.core, self.at + self.step - self.step * s)
        return self.remote(self.out.at[where], self.out.at[where], self.back_send.at[r, s], self.back_recv.at[r, s], self.mate)

    def back_arrival(self, r, s):
        where = self.rows(r, 1 - self.core, self.at - self.step + self.step * s)
        return self.remote(self.out.at[where], self.out.at[where], self.back_send.at[r, s], self.back_recv.at[r, s], self.mate)

    def launch(self, r):
        for s in range(self.chips):
            self.pair_copy(r, s).start()

    def advance(self, r, s):
        chips = self.chips
        if s < chips:
            chunk = self.at - self.step * s
            self.pair_copy(r, s, -1).wait_recv()
            total = self.g[self.rows(r, self.core, chunk), :] + self.pair_buf[self.slot(r, chunk), :]
            if s > 0:
                self.rs_copy(r, s - 1).wait_recv()
                total = total + self.ring_buf[self.landing(r, s - 1), :]
            if s < chips - 1:
                self.acc[self.slot(r, chunk), :] = total
                self.rs_copy(r, s).start()
            else:
                self.out[self.rows(r, self.core, chunk), :] = total
                self.ag_copy(r, 0, 1).start()
                self.back_copy(r, 0).start()
        else:
            s -= chips
            self.ag_copy(r, s, 0).wait_recv()
            if s < chips - 2:
                self.ag_copy(r, s + 1, 1).start()
            self.back_copy(r, s + 1).start()

    def finish(self, r):
        for s in range(self.chips):
            self.pair_copy(r, s).wait_send()
            self.back_copy(r, s).wait_send()
            self.back_arrival(r, s).wait_recv()
            if s < self.chips - 1:
                self.rs_copy(r, s).wait_send()
                self.ag_copy(r, s, 1).wait_send()


def whole_step(
    grad_scale, chips, spot, rounds, win_cols,
    features, g1_in, fine_in, fine_out, g2_in, expand, contract, gm_in, merge, gc_in, coarse_in, coarse_out, cotangent,
    out_ref, dx_ref, sum_ref,
    f_ref, g1_ref, fin, fout, g2_ref, we, wc, gm_ref, wm, gc_ref, cin, cout, cot_ref,
    f_halo, cot_halo, mid_halo, prefix,
    cells, x_ref, qkv_ref, w_ref, ctx_ref, dqkv_ref, d_all,
    mid_ref, dmid_ref, out_frame, dx_frame, coarse_cells, quads, h_ref, act_ref,
    pack_ref, pair_buf, acc, ring_buf,
    load_sem, halo_send, halo_recv, local_sem, *ring_sems,
):
    height, breadth, cf = f_ref.shape
    cc = cot_ref.shape[2]
    low = cot_ref.shape[0]
    heads, coarse_heads = cf // HEAD_DIM, cc // HEAD_DIM
    win_rows = height // WIN
    n = 2 * chips
    me = lax.axis_index("rows")
    above, below = (me + n - 1) % n, (me + 1) % n
    last = (me == n - 1).astype(jnp.int32)

    ring = Ring(chips, rounds, pack_ref, sum_ref, pair_buf, acc, ring_buf, ring_sems)
    barrier = pltpu.get_barrier_semaphore()
    for other in (above, below, ring.ahead, ring.behind, ring.mate):
        pl.semaphore_signal(barrier, inc=1, device_id={"rows": other}, device_id_type=MESH)

    sources = (features, g1_in, fine_in, fine_out, g2_in, expand, contract, gm_in, merge, gc_in, coarse_in, coarse_out, cotangent)
    targets = (f_ref, g1_ref, fin, fout, g2_ref, we, wc, gm_ref, wm, gc_ref, cin, cout, cot_ref)
    loads = {
        name: pltpu.make_async_copy(src, dst, load_sem.at[i])
        for i, (name, src, dst) in enumerate(zip(LOADS, sources, targets))
    }
    for name in LOADS:
        loads[name].start()
    pl.semaphore_wait(barrier, 5)

    def halo(i, src, dst, target):
        return ring.remote(src, dst, halo_send.at[i], halo_recv.at[i], target)

    send_f = halo(0, features.at[pl.ds(0, SHIFT)], f_halo, above)
    send_cot = halo(1, cotangent.at[pl.ds(0, SHIFT)], cot_halo, above)
    send_mid = halo(2, mid_ref.at[pl.ds(0, SHIFT)], mid_halo, above)
    send_out = halo(3, out_frame.at[pl.ds(low - SHIFT, SHIFT)], out_ref.at[pl.ds(0, SHIFT)], below)
    send_dmid = halo(4, dmid_ref.at[pl.ds(height - SHIFT, SHIFT)], prefix, below)
    send_dx = halo(5, dx_frame.at[pl.ds(height - SHIFT, SHIFT)], dx_ref.at[pl.ds(0, SHIFT)], below)
    send_f.start()
    send_cot.start()

    cells[...] = jnp.zeros_like(cells)
    quads[...] = jnp.zeros_like(quads)
    loads["g1"].wait()
    g1 = g1_ref[...].reshape(1, cf)
    rows_per = win_cols * TOK

    def window_mask(win_row, col):
        return allowed(last if win_row == win_rows - 1 else 0, int(col == win_cols - 1))

    loads["features"].wait()
    for wr in range(win_rows):
        if wr == win_rows - 1:
            send_f.wait_recv()
        fill_windows(
            cells,
            lambda r: (f_ref, r + SHIFT) if r + SHIFT < height else (f_halo, r + SHIFT - height),
            wr, win_cols, breadth,
        )
        at = slice(wr * rows_per, (wr + 1) * rows_per)
        x = cells[wr * win_cols : (wr + 1) * win_cols].reshape(rows_per, cf)
        x_ref[at, :] = x
        unit, _ = norm(x)
        u = halves(unit * g1)
        if wr == 0:
            loads["fine_in"].wait()
        parts = []
        for part in range(3):
            got = mm(u, fin[:, part * cf : (part + 1) * cf])
            qkv_ref[part, at, :] = got
            parts.append(got)
        for col in range(win_cols):
            i = wr * win_cols + col
            inside = slice(col * TOK, (col + 1) * TOK)
            w, ctx = attend(parts[0][inside], parts[1][inside], parts[2][inside], window_mask(wr, col), heads)
            w_ref[i] = w
            ctx_ref[i * TOK : (i + 1) * TOK, :] = ctx
        if wr == 0:
            loads["fine_out"].wait()
        mid = x + mm(ctx_ref[at, :], fout[...])
        cells[wr * win_cols : (wr + 1) * win_cols] = mid.reshape(win_cols, PAD, PAD, cf)
        put_windows(mid_ref, wr * WIN, cells, wr, win_cols)
        if wr == 0:
            send_mid.start()

    for name in ("g2", "gm", "gc"):
        loads[name].wait()
    g2 = g2_ref[...].reshape(1, cf)
    gmv = gm_ref[...].reshape(1, 4 * cf)
    gm = [gmv[:, k * cf : (k + 1) * cf] for k in range(4)]
    gc = gc_ref[...].reshape(1, cc)
    send_mid.wait_recv()
    for k in range(4):
        dj, di = divmod(k, 2)
        for i in range(WIN):
            r = SHIFT + 2 * i + di
            ref, r = (mid_ref, r) if r < height else (mid_halo, r - height)
            for j in range(WIN):
                at = (2 * (SHIFT + j) + dj) % breadth
                quads[k, i, j : j + 1, :] = ref[r, at : at + 1, :]
    x = quads[...].reshape(4 * TOK, cf)
    n2, r2 = norm(x)
    u2 = halves(n2 * g2)
    loads["expand"].wait()
    h = mm(u2, we[...])
    h_ref[...] = h
    act = h * (0.5 * (1.0 + lax.erf(h * 0.5**0.5)))
    act_ref[...] = act
    loads["contract"].wait()
    y = x + mm(act, wc[...], NT)
    ys = [y[k * TOK : (k + 1) * TOK] for k in range(4)]
    wide = 1.0 / (4 * cf)
    mean = sum(jnp.sum(v, axis=-1, keepdims=True) for v in ys) * wide
    ys = [v - mean for v in ys]
    rm = lax.rsqrt(sum(jnp.sum(v * v, axis=-1, keepdims=True) for v in ys) * wide + EPSILON)
    nm = [v * rm for v in ys]
    um = [halves(nm[k] * gm[k]) for k in range(4)]
    loads["merge"].wait()
    merged = sum(mm(um[k], wm[k * cf : (k + 1) * cf, :]) for k in range(4))
    nc, rc = norm(merged)
    uc = halves(nc * gc)
    loads["coarse_in"].wait()
    q, k_, v_ = (mm(uc, cin[:, p * cc : (p + 1) * cc]) for p in range(3))
    w, ctx = attend(q, k_, v_, allowed(last, 1), coarse_heads)
    loads["coarse_out"].wait()
    coarse_cells[0] = (merged + mm(ctx, cout[...])).reshape(PAD, PAD, cc)
    put_windows(out_frame, 0, coarse_cells, 0, 1)
    send_out.start()

    loads["cotangent"].wait()
    send_cot.wait_recv()
    coarse_cells[...] = jnp.zeros_like(coarse_cells)
    fill_windows(
        coarse_cells,
        lambda r: (cot_ref, r + SHIFT) if r + SHIFT < low else (cot_halo, r + SHIFT - low),
        0, 1, low,
    )
    cot = coarse_cells[0].reshape(TOK, cc)
    ch = halves(cot)
    pack_ref[spot["coarse_out"] : spot["coarse_out"] + cc, :] = mm(ctx, ch, TN) * grad_scale
    dctx = mm(ch, cout[...], NT)
    got = attend_back(dctx, q, k_, v_, w, coarse_heads)
    du = 0.0
    for p in range(3):
        dp = halves(got[p])
        top = spot["coarse_in", p]
        pack_ref[top : top + cc, :] = mm(uc, dp, TN) * grad_scale
        du += mm(dp, cin[:, p * cc : (p + 1) * cc], NT)
        if p == 0:
            ring.launch(0)
    ring.launch(1)
    ring.advance(0, 0)
    gains = spot["gains"]
    pack_ref[gains:, :] = jnp.zeros_like(pack_ref[gains:, :])
    pack_ref[gains + 3 : gains + 4, :] = jnp.sum(du * nc, axis=0, keepdims=True) * grad_scale
    dm = cot + norm_back(du * gc, nc, rc)
    mh = halves(dm)
    dn = []
    for k in range(4):
        top = spot["merge"] + k * cf
        pack_ref[top : top + cf, :] = mm(um[k], mh, TN) * grad_scale
        dk = mm(mh, wm[k * cf : (k + 1) * cf, :], NT)
        row = gains + 1 + k // 2
        pack_ref[row : row + 1, (k % 2) * cf : (k % 2 + 1) * cf] = jnp.sum(dk * nm[k], axis=0, keepdims=True) * grad_scale
        dn.append(dk * gm[k])
    ring.launch(2)
    ring.advance(1, 0)
    ring.advance(0, 1)
    m1 = sum(jnp.sum(v, axis=-1, keepdims=True) for v in dn) * wide
    m2 = sum(jnp.sum(dn[k] * nm[k], axis=-1, keepdims=True) for k in range(4)) * wide
    dy = jnp.concatenate([rm * (dn[k] - m1 - nm[k] * m2) for k in range(4)], axis=0)
    yh = halves(dy)
    dwc = mm(yh, act_ref[...], TN) * grad_scale
    top = spot["contract"]
    for p in range(dwc.shape[1] // cc):
        pack_ref[top + p * cf : top + (p + 1) * cf, :] = dwc[:, p * cc : (p + 1) * cc]
    ring.advance(2, 0)
    ring.advance(1, 1)
    ring.advance(0, 2)
    h = h_ref[...]
    slope = 0.5 * (1.0 + lax.erf(h * 0.5**0.5)) + h * (jnp.exp(-0.5 * h * h) * 0.3989422804014327)
    dh = halves(mm(yh, wc[...]) * slope)
    dwe = mm(u2, dh, TN) * grad_scale
    top = spot["expand"]
    for p in range(dwe.shape[1] // cc):
        pack_ref[top + p * cf : top + (p + 1) * cf, :] = dwe[:, p * cc : (p + 1) * cc]
    ring.launch(3)
    du2 = mm(dh, we[...], NT)
    pack_ref[gains : gains + 1, :cf] = jnp.sum(du2 * n2, axis=0, keepdims=True) * grad_scale
    quads[...] = (dy + norm_back(du2 * g2, n2, r2)).reshape(quads.shape)
    for k in range(4):
        dj, di = divmod(k, 2)
        for i in range(WIN):
            for j in range(WIN):
                at = (2 * (SHIFT + j) + dj) % breadth
                dmid_ref[2 * i + di, at : at + 1, :] = quads[k, i, j : j + 1, :]
    send_dmid.start()
    ring.advance(3, 0)
    ring.advance(2, 1)
    ring.advance(1, 2)
    ring.advance(0, 3)

    for w0 in range(cells.shape[0]):
        cells[w0, WIN:, :, :] = jnp.zeros_like(cells[w0, WIN:, :, :])
        cells[w0, :, WIN:, :] = jnp.zeros_like(cells[w0, :, WIN:, :])
    for wr in reversed(range(win_rows)):
        if wr == 0:
            send_dmid.wait_recv()
        fill_windows(
            cells, lambda r: (dmid_ref, r - SHIFT) if r >= SHIFT else (prefix, r), wr, win_cols, breadth
        )
        at = slice(wr * rows_per, (wr + 1) * rows_per)
        d = cells[wr * win_cols : (wr + 1) * win_cols].reshape(rows_per, cf)
        d_all[at, :] = d
        unit, scale = norm(x_ref[at, :])
        dctx = mm(d, fout[...], NT)
        for col in range(win_cols):
            i = wr * win_cols + col
            inside = slice(i * TOK, (i + 1) * TOK)
            got = attend_back(
                dctx[col * TOK : (col + 1) * TOK], qkv_ref[0, inside, :], qkv_ref[1, inside, :], qkv_ref[2, inside, :], w_ref[i], heads
            )
            for part in range(3):
                dqkv_ref[part, inside, :] = got[part]
        du = 0.0
        for part in range(3):
            du += mm(dqkv_ref[part, at, :], fin[:, part * cf : (part + 1) * cf], NT)
        gain_part = jnp.sum(du * unit, axis=0, keepdims=True)
        gain_one = gain_part if wr == win_rows - 1 else gain_one + gain_part
        cells[wr * win_cols : (wr + 1) * win_cols] = (d + norm_back(du * g1, unit, scale)).reshape(win_cols, PAD, PAD, cf)
        put_windows(dx_frame, wr * WIN, cells, wr, win_cols)
        if wr == win_rows - 1:
            send_dx.start()
        shift = win_rows - 1 - wr
        for r in range(4):
            ring.advance(3 - r, 1 + shift + r)
    unit, _ = norm(x_ref[...])
    u = halves(unit * g1)
    weight = [mm(u, dqkv_ref[part], TN) * grad_scale for part in range(3)]
    dwout = mm(ctx_ref[...], d_all[...], TN) * grad_scale
    top = spot["fine"]
    pack_ref[top : top + cf, :] = jnp.concatenate(weight[:2], axis=1)
    pack_ref[top + cf : top + 2 * cf, :] = jnp.concatenate([weight[2], dwout], axis=1)
    pack_ref[gains + 4 : gains + 5, :cf] = gain_one * grad_scale
    ring.launch(4)

    keep_out = pltpu.make_async_copy(
        out_frame.at[pl.ds(0, low - SHIFT)], out_ref.at[pl.ds(SHIFT, low - SHIFT)], local_sem.at[0]
    )
    keep_dx = pltpu.make_async_copy(
        dx_frame.at[pl.ds(0, height - SHIFT)], dx_ref.at[pl.ds(SHIFT, height - SHIFT)], local_sem.at[1]
    )
    keep_out.start()
    keep_dx.start()
    count = len(rounds)
    done = [1 + win_rows + 3 - r for r in range(4)] + [0]
    steps = 2 * chips - 1
    todo = sorted(((s - done[r] + 0.5) / (steps - done[r]), r, s) for r in range(count) for s in range(done[r], steps))
    for _, r, s in todo:
        ring.advance(r, s)
    for r in range(count):
        ring.finish(r)
    keep_out.wait()
    keep_dx.wait()
    for copy in (send_f, send_cot, send_mid, send_out, send_dmid, send_dx):
        copy.wait_send()
    send_out.wait_recv()
    send_dx.wait_recv()


def unpack(spot, cf, cc, sum_ref, out_ref, dx_ref, *rest):
    (coarse_out, grad_features, g1, fine_in, fine_out, g2, expand, contract, gm, merge, gc, coarse_in, coarse_proj) = rest[:13]
    sems = rest[13]
    moves = [
        (out_ref, coarse_out),
        (dx_ref, grad_features),
        (sum_ref.at[pl.ds(spot["merge"], 4 * cf)], merge),
        (sum_ref.at[pl.ds(spot["coarse_out"], cc)], coarse_proj),
    ]
    for name, into in (("coarse_in", coarse_in), ("expand", expand), ("contract", contract)):
        size = into.shape[0]
        for p in range(into.shape[1] // cc):
            at = spot[name, p] if (name, p) in spot else spot[name] + p * size
            moves.append((sum_ref.at[pl.ds(at, size)], into.at[:, pl.ds(p * cc, cc)]))
    copies = [pltpu.make_async_copy(src, dst, sems.at[i]) for i, (src, dst) in enumerate(moves)]
    for copy in copies:
        copy.start()
    top = spot["fine"]
    fine_in[:, :cc] = sum_ref[top : top + cf, :]
    fine_in[:, cc:] = sum_ref[top + cf : top + 2 * cf, :cf]
    fine_out[...] = sum_ref[top + cf : top + 2 * cf, cf:]
    gains = spot["gains"]
    g1[...] = sum_ref[gains + 4 : gains + 5, :cf].reshape(g1.shape)
    g2[...] = sum_ref[gains : gains + 1, :cf].reshape(g2.shape)
    gm[...] = jnp.concatenate([sum_ref[gains + 1 : gains + 2, :], sum_ref[gains + 2 : gains + 3, :]], axis=1).reshape(gm.shape)
    gc[...] = sum_ref[gains + 3 : gains + 4, :].reshape(gc.shape)
    for copy in copies:
        copy.wait()


def shards(
    features,
    fine_gain_one,
    fine_project_in,
    fine_project_out,
    fine_gain_two,
    fine_expand,
    fine_contract,
    merge_gain,
    merge_weight,
    coarse_gain,
    coarse_project_in,
    coarse_project_out,
    cotangent,
):
    devices = lax.axis_size("rows")
    chips = devices // 2
    height, breadth, cf = features.shape
    low, narrow, cc = cotangent.shape
    units = fine_expand.shape[1]
    assert low == narrow == WIN and cc == 2 * cf and units % cc == 0
    grad_scale = 1.0 / (devices * low * narrow) ** 0.5
    win_rows, win_cols = height // WIN, breadth // WIN
    count = win_rows * win_cols
    heads = cf // HEAD_DIM
    tokens = count * TOK
    vmem = pl.BlockSpec(memory_space=pltpu.VMEM)
    anywhere = pl.BlockSpec(memory_space=pl.ANY)

    def shape(*dims):
        return jax.ShapeDtypeStruct(dims, F32)

    def limit(mib):
        return pltpu.CompilerParams(vmem_limit_bytes=mib * 2**20)

    grain = 8 * devices
    spot, rounds, rows = {}, [], 0
    strips = units // cc * cf
    plan = (
        (("coarse_out", cc), (("coarse_in", 0), cc)),
        ((("coarse_in", 1), cc), (("coarse_in", 2), cc)),
        (("merge", 4 * cf),),
        (("contract", strips), ("expand", strips)),
        (("fine", 2 * cf), ("gains", 8)),
    )
    for group in plan:
        top = rows
        for name, size in group:
            spot[name] = rows
            rows += size
        padded = -(-(rows - top) // grain) * grain
        rounds.append((top, padded // devices))
        rows = top + padded
    total = rows
    scratch = [
        pltpu.VMEM(a.shape, F32)
        for a in (
            features, fine_gain_one, fine_project_in, fine_project_out, fine_gain_two, fine_expand, fine_expand,
            merge_gain, merge_weight, coarse_gain, coarse_project_in, coarse_project_out, cotangent,
        )
    ]
    scratch += [
        pltpu.VMEM(dims, F32)
        for dims in (
            (SHIFT, breadth, cf),
            (SHIFT, narrow, cc),
            (SHIFT, breadth, cf),
            (SHIFT, breadth, cf),
            (count, PAD, PAD, cf),
            (tokens, cf),
            (3, tokens, cf),
            (count, heads * TOK, TOK),
            (tokens, cf),
            (3, tokens, cf),
            (tokens, cf),
            (height, breadth, cf),
            (height, breadth, cf),
            (low, narrow, cc),
            (height, breadth, cf),
            (1, PAD, PAD, cc),
            (4, PAD, PAD, cf),
            (4 * TOK, units),
            (4 * TOK, units),
            (total, cc),
            (total // 2, cc),
            (total // 2, cc),
            (total // 2, cc),
        )
    ]
    dma = pltpu.SemaphoreType.DMA
    scratch += [dma((len(LOADS),)), dma((6,)), dma((6,)), dma((2,))]
    scratch += [dma((len(rounds), chips)) for _ in range(8)]
    out_slab, dx, summed = pl.pallas_call(
        functools.partial(whole_step, grad_scale, chips, spot, rounds, win_cols),
        out_shape=(shape(low, narrow, cc), shape(height, breadth, cf), shape(total, cc)),
        in_specs=[pl.BlockSpec(memory_space=pltpu.HBM)] * len(LOADS),
        out_specs=(vmem,) * 3,
        scratch_shapes=scratch,
        compiler_params=pltpu.CompilerParams(
            collective_id=0, has_side_effects=True, vmem_limit_bytes=36 * 2**20
        ),
        name="whole_step",
    )(
        *(
            pltpu.with_memory_space_constraint(a, pltpu.HBM)
            for a in (
                features, fine_gain_one, fine_project_in, fine_project_out, fine_gain_two, fine_expand, fine_contract.T,
                merge_gain, merge_weight, coarse_gain, coarse_project_in, coarse_project_out, cotangent,
            )
        )
    )
    final = pl.pallas_call(
        functools.partial(unpack, spot, cf, cc),
        out_shape=(
            shape(low, narrow, cc),
            shape(height, breadth, cf),
            shape(cf),
            shape(cf, 3 * cf),
            shape(cf, cf),
            shape(cf),
            shape(cf, units),
            shape(cf, units),
            shape(4 * cf),
            shape(4 * cf, cc),
            shape(cc),
            shape(cc, 3 * cc),
            shape(cc, cc),
        ),
        in_specs=[vmem] * 3,
        out_specs=(anywhere, anywhere, vmem, vmem, vmem, vmem, anywhere, anywhere, vmem, anywhere, vmem, anywhere, anywhere),
        scratch_shapes=[pltpu.SemaphoreType.DMA((4 + 3 + 2 * (units // cc),))],
        compiler_params=limit(20),
        name="unpack",
    )(summed, out_slab, dx)
    final = list(final)
    final[7] = final[7].T
    return tuple(final)


def solution(mesh):
    tokens = P(("groups", "rows"), None, None)
    vector, matrix = P("groups"), P("groups", None)
    in_specs = (tokens,) + (P(),) * 11 + (tokens,)
    out_specs = (
        tokens,
        tokens,
        vector,
        matrix,
        matrix,
        vector,
        matrix,
        matrix,
        vector,
        matrix,
        vector,
        matrix,
        matrix,
    )
    return jax.shard_map(shards, mesh=mesh, in_specs=in_specs, out_specs=out_specs, check_vma=False)
```
